32 devices in a mesh: groups: 1, row: 8 (over z, y), col: 4 (over x, core).
Axes of the slice: x: 2, y: 2, z: 4, core: 2. Of those that a mesh axis runs over, the one named last changes fastest.
Arguments:
- activations: bfloat16 [1024, 16384], P('groups', ('row', 'col')), may hold values from -2.5 to 2.5
- token_ids: int32 [1024], P('groups'), may hold values from 0 to 128255
- initial: float32 [16384, 256], P(('groups', 'row', 'col')), may hold values from -6 to 6
- block_mask: int32 [128, 2], P('groups'), may hold values 0 or 1
Outputs:
- gram: float32 [8, 4, 512, 16384], P('groups', 'col', None, 'row')
- repaired: float32 [16384, 256], P(('groups', 'row', 'col'))
The draws below stay inside these ranges and needn't reach their ends.
All inputs are finite; a program needn't handle non-finite values.
Results may differ from the reference program's by a relative error of at most 0.0003.
Values may be sent and summed in bfloat16 or wider, within the bound.
No kernel may reach another device: no remote copies, remote signals or barrier semaphores. Data moves between devices by JAX's collectives and lax.ppermute only.
A program may use at most 128 MiB of HBM per device.

```python
import math
import jax
import jax.numpy as jnp
import numpy as np
from jax import lax

D = 16384
VOCAB = 128256
ROWS = 1024
OUTC = 256
BLOCK = 128
ITERS = 2
SHARD = 512
N_ROW = 8
N_COL = 4


def draw_activations(key, part):
    entry_key = jax.random.fold_in(key, 11)
    values = jnp.clip(jax.random.normal(entry_key, (ROWS, D), jnp.float32), -2.5, 2.5)
    return values.astype(jnp.bfloat16)


def set_ends(result, rng, least, top_value):
    spot = [jax.random.randint(jax.random.fold_in(rng, axis), (), 0, length) for axis, length in enumerate(result.shape)]
    longest = result.shape.index(max(result.shape))
    next_to = spot[:longest] + [(spot[longest] + 1) % result.shape[longest]] + spot[longest + 1:]
    return result.at[tuple(spot)].set(least).at[tuple(next_to)].set(top_value)


def levels(key, extent, split, smallest, high):
    gain, own = 1.0, jax.random.fold_in(key, 6)
    for dim, blocks in split:
        steps = jnp.exp(jax.random.uniform(jax.random.fold_in(own, dim), (blocks,), jnp.float32, smallest / len(split), high / len(split)))
        gain = gain * jnp.repeat(steps, extent[dim] // blocks).reshape([-1 if axis == dim else 1 for axis in range(len(extent))])
    return gain


def skewed_wide(rng, shape, count, slope):
    loads = [min(1 << octave, count + 1 - (1 << octave)) * (1 << 20) // math.isqrt((1 << octave) ** slope) + 1 for octave in range((count + 1).bit_length()) if 1 << octave <= count]
    deviation = 1 + sum(loads) // (1 << 30)
    listing = np.cumsum(np.array([max(1, weight // deviation) for weight in loads]))
    ticket = jax.random.randint(jax.random.fold_in(rng, 1), shape, 0, int(listing[len(loads) - 1]))
    start = jnp.left_shift(1, jnp.searchsorted(jnp.asarray(listing, jnp.int32), ticket, side="right").astype(jnp.int32))
    standing = start - 1 + jax.random.randint(jax.random.fold_in(rng, 4), shape, 0, 1 << 30) % jnp.minimum(start, count + 1 - start)
    return jax.random.permutation(jax.random.fold_in(rng, 2), count)[standing].astype(jnp.int32)


def noise(own_key, dims, spread, most, split=(), held_as=jnp.bfloat16):
    drawn = jax.random.normal(own_key, dims, jnp.float32) * spread
    if len(split) > 0:
        drawn = levels(own_key, dims, split, -0.22, 0.18) * drawn
    return jnp.clip(drawn, min=-most, max=most).astype(held_as)


def setup_inputs(seed: int = 0, part: int = 0) -> dict:
    splits = jax.random.split(jax.random.key(seed), 5)
    part_splits = jax.random.split(jax.random.fold_in(splits[4], part), 5)
    activations = draw_activations(jax.random.fold_in(jax.random.fold_in(splits[4], part), 71), part)
    token_ids = set_ends(skewed_wide(part_splits[1], (ROWS,), VOCAB, 2), jax.random.fold_in(part_splits[1], 3), 0, VOCAB - 1).astype(jnp.int32)
    initial = noise(part_splits[2], (D, OUTC), 1.0, 6.0, ((0, 32),), jnp.float32)
    block_mask = set_ends((jax.random.randint(part_splits[3], (D // BLOCK, OUTC // BLOCK), 0, 2) < 1).astype(jnp.int32), jax.random.fold_in(part_splits[3], 1), 0, 1)
    return dict(activations=activations, token_ids=token_ids, initial=initial, block_mask=block_mask)


def reference(activations, token_ids, initial, block_mask):
    matches = (token_ids[:, None] == token_ids[None, :]).astype(jnp.float32)
    weights = 1.0 / lax.optimization_barrier(jnp.sum(matches, axis=1))
    weighted = (activations.astype(jnp.float32) * weights[:, None]).astype(jnp.bfloat16)
    gram_full = lax.dot_general(weighted.astype(jnp.float32), activations.astype(jnp.float32), (((0,), (0,)), ((), ())), precision=lax.Precision.HIGHEST) * (1.0 / ROWS)
    mask_full = jnp.repeat(jnp.repeat(block_mask.astype(jnp.float32), BLOCK, axis=0), BLOCK, axis=1)
    step_size = ROWS / (D + 2.0 * math.sqrt(D * ROWS) + ROWS)
    current = mask_full * initial
    for iteration in range(ITERS):
        change_now = current - initial
        pulled = jnp.dot(gram_full, change_now, precision=lax.Precision.HIGHEST)
        current = mask_full * (current - step_size * pulled)
    return (gram_full.reshape(N_ROW, N_COL, SHARD, D), current)
```

```python
import functools
import math

import jax
import jax.numpy as jnp
from jax import lax
from jax.experimental import pallas as pl
from jax.experimental.pallas import tpu as pltpu
from jax.sharding import PartitionSpec as P

BLOCK = 128
PARTS = 2


def split3(value):
    high = value.astype(jnp.bfloat16)
    rest = value - high.astype(jnp.float32)
    middle = rest.astype(jnp.bfloat16)
    low = (rest - middle.astype(jnp.float32)).astype(jnp.bfloat16)
    return jnp.concatenate([high, middle, low], axis=0)


def sum3(value):
    third = value.shape[0] // 3
    return value[:third] + (value[third : 2 * third] + value[2 * third :])


def nt_dot(left, right):
    return lax.dot_general(left, right, (((1,), (1,)), ((), ())), preferred_element_type=jnp.float32)


def project_kernel(first_ref, mask_ref, initial_ref, act_ref, out_ref):
    features, columns = initial_ref.shape
    step = min(BLOCK, features)
    rows = []
    for low in range(0, features, step):
        blocks = []
        for o in range(columns // BLOCK):
            kept = mask_ref[first_ref[0] + low // step, o].astype(jnp.float32) - 1.0
            blocks.append(initial_ref[low : low + step, o * BLOCK : (o + 1) * BLOCK] * kept)
        rows.append(jnp.concatenate(blocks, axis=1))
    change = jnp.concatenate(rows, axis=0)
    out_ref[...] = sum3(nt_dot(split3(change.T), act_ref[...]))


def project(initial, act, block_mask, first_block):
    return pl.pallas_call(
        project_kernel,
        out_shape=jax.ShapeDtypeStruct((initial.shape[1], act.shape[0]), jnp.float32),
        in_specs=[
            pl.BlockSpec(memory_space=pltpu.SMEM),
            pl.BlockSpec(memory_space=pltpu.SMEM),
            pl.BlockSpec(memory_space=pltpu.VMEM),
            pl.BlockSpec(memory_space=pltpu.VMEM),
        ],
        out_specs=pl.BlockSpec(memory_space=pltpu.VMEM),
        compiler_params=pltpu.CompilerParams(vmem_limit_bytes=16 << 20),
        name="project",
    )(first_block, block_mask, initial, act)


def step_kernel(total_ref, weighted_ref, act_ref, mask_ref, out_ref, split_ref):
    tile = pl.program_id(0)

    @pl.when(tile == 0)
    def _():
        split_ref[...] = split3(total_ref[...])
        out_ref[...] = jnp.zeros_like(out_ref)

    pulled = sum3(jnp.dot(split_ref[...], weighted_ref[...], preferred_element_type=jnp.float32))
    out_ref[...] += sum3(nt_dot(split3(pulled * mask_ref[...]), act_ref[...]))


def masked_step(total, weighted_panel, act_panel, mask_panel):
    columns, rows = total.shape
    features = act_panel.shape[1]
    tile = min(512, features)
    return pl.pallas_call(
        step_kernel,
        grid=(features // tile,),
        out_shape=jax.ShapeDtypeStruct((columns, rows), jnp.float32),
        in_specs=[
            pl.BlockSpec((columns, rows), lambda i: (0, 0)),
            pl.BlockSpec((rows, tile), lambda i: (0, i)),
            pl.BlockSpec((rows, tile), lambda i: (0, i)),
            pl.BlockSpec((1, tile), lambda i: (0, i)),
        ],
        out_specs=pl.BlockSpec((columns, rows), lambda i: (0, 0)),
        scratch_shapes=[pltpu.VMEM((3 * columns, rows), jnp.bfloat16)],
        compiler_params=pltpu.CompilerParams(vmem_limit_bytes=16 << 20),
        name="masked_step",
    )(total, weighted_panel, act_panel, mask_panel)


def pull_kernel(total_ref, weighted_ref, out_ref, split_ref):
    @pl.when(pl.program_id(0) == 0)
    def _():
        split_ref[...] = split3(total_ref[...])

    out_ref[...] = sum3(jnp.dot(split_ref[...], weighted_ref[...], preferred_element_type=jnp.float32))


def pull(total, weighted_panel):
    columns, rows = total.shape
    features = weighted_panel.shape[1]
    tile = min(512, features)
    return pl.pallas_call(
        pull_kernel,
        grid=(features // tile,),
        out_shape=jax.ShapeDtypeStruct((columns, features), jnp.float32),
        in_specs=[
            pl.BlockSpec((columns, rows), lambda i: (0, 0)),
            pl.BlockSpec((rows, tile), lambda i: (0, i)),
        ],
        out_specs=pl.BlockSpec((columns, tile), lambda i: (0, i)),
        scratch_shapes=[pltpu.VMEM((3 * columns, rows), jnp.bfloat16)],
        compiler_params=pltpu.CompilerParams(vmem_limit_bytes=16 << 20),
        name="pull",
    )(total, weighted_panel)


def gram_kernel(scale, parts, index_ref, *refs):
    weighted = refs[:parts]
    panel_ref = refs[parts]
    out_ref = refs[-1]
    height = weighted[0].shape[0]
    for i in range(parts):
        out_ref[0, 0, i * height : (i + 1) * height, :] = (
            jnp.dot(weighted[i][...], panel_ref[...], preferred_element_type=jnp.float32) * scale
        )


def gram_block(buffer, index, slot, pieces, panel, blocks):
    height, rows = pieces[0].shape
    parts = len(pieces)
    features = panel.shape[1]
    tile = min(512, features)
    shape = (blocks, 1, parts * height, features)
    in_specs = [pl.BlockSpec((height, rows), lambda i, idx: (0, 0)) for _ in pieces]
    in_specs.append(pl.BlockSpec((rows, tile), lambda i, idx: (0, i)))
    operands = [index, *pieces, panel]
    aliases = {}
    if buffer is not None:
        in_specs.append(pl.BlockSpec(memory_space=pl.ANY))
        aliases = {len(operands): 0}
        operands.append(buffer)
    return pl.pallas_call(
        functools.partial(gram_kernel, 1.0 / rows, parts),
        grid_spec=pltpu.PrefetchScalarGridSpec(
            num_scalar_prefetch=1,
            grid=(features // tile,),
            in_specs=in_specs,
            out_specs=pl.BlockSpec((1, 1, parts * height, tile), lambda i, idx: (idx[slot], 0, 0, i)),
        ),
        out_shape=jax.ShapeDtypeStruct(shape, jnp.float32),
        input_output_aliases=aliases,
        compiler_params=pltpu.CompilerParams(vmem_limit_bytes=24 << 20),
        cost_estimate=pl.CostEstimate(
            flops=2 * parts * height * rows * features,
            bytes_accessed=4 * parts * height * features + 2 * rows * (features + parts * height),
            transcendentals=0,
        ),
        name=f"gram_{slot}",
    )(*operands)


def exchange(value, axis, bit):
    size = lax.axis_size(axis)
    return lax.ppermute(value, axis, [(i, i ^ bit) for i in range(size)])


def halve(value, axis, bit):
    half = value.shape[0] // 2
    mine = (lax.axis_index(axis) // bit) % 2
    keep = lax.dynamic_slice_in_dim(value, mine * half, half, 0)
    give = lax.dynamic_slice_in_dim(value, (1 - mine) * half, half, 0)
    return keep + exchange(give, axis, bit)


def unite(value, axis, bit):
    other = exchange(value, axis, bit)
    first = (lax.axis_index(axis) // bit) % 2 == 0
    return jnp.concatenate([jnp.where(first, value, other), jnp.where(first, other, value)], axis=0)


def bits(size):
    return [1 << i for i in range(size.bit_length() - 1)]


def row_sum(value, row_count):
    scatter = value.shape[0] % 16 == 0
    if scatter:
        value = halve(value, "row", 1)
    else:
        value = value + exchange(value, "row", 1)
    for bit in bits(row_count)[1:]:
        value = value + exchange(value, "row", bit)
    return unite(value, "row", 1) if scatter else value


def shards(activations, token_ids, initial, block_mask):
    rows, features = activations.shape
    row_count, col_count = lax.axis_size("row"), lax.axis_size("col")
    columns = initial.shape[1]
    row, col = lax.axis_index("row"), lax.axis_index("col")
    depth = row_count * col_count * features
    step_size = rows / (depth + 2.0 * math.sqrt(depth * rows) + rows)

    matches = (token_ids[:, None] == token_ids[None, :]).astype(jnp.float32)
    weights = 1.0 / jnp.sum(matches, axis=1)

    weighted_t = (activations.astype(jnp.float32) * weights[:, None]).astype(jnp.bfloat16).T
    order = list(range(0, row_count, 2)) + list(range(row_count - 1, 0, -2))
    forward = [(order[i], order[(i + 1) % row_count]) for i in range(row_count)]
    backward = [(b, a) for a, b in forward]
    place = [order.index(r) for r in range(row_count)]
    sources = [[order[(place[r] - s) % row_count] for s in range(row_count)] for r in range(row_count)]
    index = jnp.array(sources, jnp.int32)[row]
    height = features // PARTS
    pieces = [weighted_t[i * height : (i + 1) * height] for i in range(PARTS)]
    held = {0: pieces}
    ahead, behind = list(pieces), list(pieces)
    for step in range(1, row_count // 2 + 1):
        last = step == row_count // 2
        for i in range(PARTS):
            if not last or i < PARTS // 2:
                ahead[i] = lax.ppermute(ahead[i], "row", forward)
            if not last or i >= PARTS // 2:
                behind[i] = lax.ppermute(behind[i], "row", backward)
        if last:
            held[step] = ahead[: PARTS // 2] + behind[PARTS // 2 :]
        else:
            held[step] = list(ahead)
            held[row_count - step] = list(behind)

    panel = activations
    for bit in reversed(bits(col_count)):
        other = exchange(panel, "col", bit)
        low = (col // bit) % 2 == 0
        if bit == bits(col_count)[-1]:
            panel = jnp.stack([jnp.where(low, panel, other), jnp.where(low, other, panel)])
        else:
            panel = jnp.stack([jnp.where(low, panel, other), jnp.where(low, other, panel)], axis=-3)
    panel = panel.reshape(col_count, rows, features).transpose(1, 0, 2).reshape(rows, col_count * features)
    weighted_panel = (panel.astype(jnp.float32) * weights[:, None]).astype(jnp.bfloat16)

    first_block = ((row * col_count + col) * features // BLOCK).astype(jnp.int32).reshape(1)
    total = project(initial, activations, block_mask, first_block)
    for bit in bits(col_count):
        total = halve(total, "col", bit)
    first_column = 0
    width = columns
    for bit in bits(col_count):
        width //= 2
        first_column = first_column + ((col // bit) % 2) * width
    total = row_sum(total, row_count)
    panel_blocks = col_count * features // BLOCK
    mask_column = lax.dynamic_slice(
        block_mask, (row * panel_blocks, first_column // BLOCK), (panel_blocks, 1)
    )
    mask_panel = jnp.repeat(mask_column.astype(jnp.float32).reshape(panel_blocks), BLOCK)[None, :]
    moved = row_sum(masked_step(total, weighted_panel, panel, mask_panel), row_count)
    both = total + (total - (step_size / rows) * moved)
    change = pull(both, weighted_panel)
    change = change.reshape(width, col_count, features)
    for bit in reversed(bits(col_count)):
        half = change.shape[1] // 2
        mine = (col // bit) % 2
        keep = lax.dynamic_slice_in_dim(change, mine * half, half, 1)
        give = lax.dynamic_slice_in_dim(change, (1 - mine) * half, half, 1)
        got = exchange(give, "col", bit)
        change = jnp.concatenate(
            [jnp.where(mine == 0, keep, got), jnp.where(mine == 0, got, keep)], axis=0
        )
    change = change.reshape(columns, features).T
    local_blocks = max(1, features // BLOCK)
    local_mask = lax.dynamic_slice(block_mask, (first_block[0], 0), (local_blocks, columns // BLOCK))
    local_mask = jnp.repeat(local_mask.astype(jnp.float32), features // local_blocks, axis=0)
    local_mask = jnp.repeat(local_mask, BLOCK, axis=1)
    repaired = local_mask * (initial - (step_size / rows) * change)

    gram = None
    arrival = [0]
    for step in range(1, row_count // 2 + 1):
        arrival += [step] if step == row_count // 2 else [step, row_count - step]
    for slot in arrival:
        gram = gram_block(gram, index, slot, held[slot], panel, row_count)
    return gram, repaired


def solution(mesh):
    in_specs = (
        P("groups", ("row", "col")),
        P("groups"),
        P(("groups", "row", "col"), None),
        P("groups", None),
    )
    out_specs = (P("groups", "col", None, "row"), P(("groups", "row", "col"), None))
    return jax.shard_map(shards, mesh=mesh, in_specs=in_specs, out_specs=out_specs, check_vma=False)
```

```python
import functools
import math

import jax
import jax.numpy as jnp
from jax import lax
from jax.experimental import pallas as pl
from jax.experimental.pallas import tpu as pltpu
from jax.sharding import PartitionSpec as P


BLOCK = 128
SLOTS = [0, 2, 3, 5, 4, 6, 10, 7, 8, 10, 11]


SMEM = pl.BlockSpec(memory_space=pltpu.SMEM)
VMEM = pl.BlockSpec(memory_space=pltpu.VMEM)
ANY = pl.BlockSpec(memory_space=pl.ANY)


def split3(value):
    high = value.astype(jnp.bfloat16)
    rest = value - high.astype(jnp.float32)
    middle = rest.astype(jnp.bfloat16)
    low = (rest - middle.astype(jnp.float32)).astype(jnp.bfloat16)
    return jnp.concatenate([high, middle, low], axis=0)


def sum3(value):
    third = value.shape[0] // 3
    return value[:third] + (value[third : 2 * third] + value[2 * third :])


def nt_dot(left, right):
    return lax.dot_general(left, right, (((1,), (1,)), ((), ())), preferred_element_type=jnp.float32)


def dot(left, right):
    return jnp.dot(left, right, preferred_element_type=jnp.float32)


def mib(count):
    return pltpu.CompilerParams(vmem_limit_bytes=count << 20)


def keep_give(value, mine, keep_ref, give_ref):
    half = value.shape[0] // 2
    low, high = value[:half], value[half:]
    first = mine == 0
    keep_ref[...] = jnp.where(first, low, high)
    give_ref[...] = jnp.where(first, high, low)


def lanes(column, width):
    if width <= column.shape[1]:
        return column[:, :width]
    return jnp.concatenate([column] * (width // column.shape[1]), axis=1)


def start_kernel(first_ref, mine_ref, mask_ref, ids_ref, act_in, initial_in, *refs):
    keep_ref, give_ref, act_ref, column_ref = refs[:4]
    piece_refs, (initial_ref, sems) = refs[4:-2], refs[-2:]
    act_copy = pltpu.make_async_copy(act_in, act_ref, sems.at[0])
    initial_copy = pltpu.make_async_copy(initial_in, initial_ref, sems.at[1])
    act_copy.start()
    initial_copy.start()
    rows = ids_ref.shape[1]
    ids = ids_ref[...].astype(jnp.float32)
    ids_column = jnp.broadcast_to(ids, (BLOCK, rows)).T
    counts = []
    for low in range(0, rows, BLOCK):
        same = jnp.where(ids_column == ids[:, low : low + BLOCK], 1.0, 0.0)
        counts.append(jnp.sum(same, axis=0, keepdims=True))
    weights = 1.0 / jnp.concatenate(counts, axis=1)
    column_ref[...] = jnp.broadcast_to(weights, (BLOCK, rows)).T
    initial_copy.wait()
    features, columns = initial_ref.shape
    step = min(BLOCK, features)
    stripes = []
    for low in range(0, features, step):
        blocks = []
        for o in range(columns // BLOCK):
            kept = mask_ref[o, first_ref[0] + low // step].astype(jnp.float32) - 1.0
            blocks.append(initial_ref[low : low + step, o * BLOCK : (o + 1) * BLOCK] * kept)
        stripes.append(jnp.concatenate(blocks, axis=1))
    change = split3(jnp.concatenate(stripes, axis=0).T)
    act_copy.wait()
    keep_give(sum3(nt_dot(change, act_ref[...])), mine_ref[0], keep_ref, give_ref)
    weighted = (act_ref[...].astype(jnp.float32).T * weights).astype(jnp.bfloat16)
    low = 0
    for piece_ref in piece_refs:
        piece_ref[...] = weighted[low : low + piece_ref.shape[0]]
        low += piece_ref.shape[0]


def start(first_block, mine, mask_t, token_ids, act, initial, heights):
    rows = act.shape[0]
    half = jax.ShapeDtypeStruct((initial.shape[1] // 2, rows), jnp.float32)
    shapes = [half, half, jax.ShapeDtypeStruct(act.shape, act.dtype)]
    shapes += [jax.ShapeDtypeStruct((rows, BLOCK), jnp.float32)]
    shapes += [jax.ShapeDtypeStruct((h, rows), jnp.bfloat16) for h in heights]
    return pl.pallas_call(
        start_kernel,
        out_shape=tuple(shapes),
        in_specs=[SMEM, SMEM, SMEM, VMEM, ANY, ANY],
        out_specs=(VMEM,) * len(shapes),
        scratch_shapes=[pltpu.VMEM(initial.shape, jnp.float32), pltpu.SemaphoreType.DMA((2,))],
        compiler_params=mib(24),
        name="start",
    )(first_block.reshape(1), mine.reshape(1), mask_t, token_ids[None, :], act, initial)


def fold_kernel(where_ref, held_ref, got_ref, keep_ref, give_ref):
    keep_give(held_ref[...] + got_ref[...], where_ref[0], keep_ref, give_ref)


def fold(held, got, mine):
    half = jax.ShapeDtypeStruct((held.shape[0] // 2, held.shape[1]), jnp.float32)
    return pl.pallas_call(
        fold_kernel,
        out_shape=(half, half),
        in_specs=[SMEM, VMEM, VMEM],
        out_specs=(VMEM, VMEM),
        compiler_params=mib(4),
        name="fold",
    )(mine.reshape(1), held, got)


def step_kernel(spots, given, where_ref, mask_ref, column_ref, *refs):
    total_refs, refs = refs[:given], refs[given:]
    count = len(spots)
    act_ins, out_refs, (act_refs, sems) = refs[:count], refs[count:-2], refs[-2:]
    copies = [pltpu.make_async_copy(act_ins[j], act_refs.at[j], sems.at[j]) for j in range(count)]
    for copy in copies:
        copy.start()
    features = act_refs.shape[2]
    step = min(BLOCK, features)
    pieces = split3(jnp.concatenate([ref[...] for ref in total_refs], axis=0))
    weights = lanes(column_ref[...], features)
    moved = None
    for j in range(count):
        copies[j].wait()
        act = act_refs[j]
        pulled = sum3(dot(pieces, (act.astype(jnp.float32) * weights).astype(jnp.bfloat16)))
        masked = []
        for low in range(0, features, step):
            kept = mask_ref[where_ref[spots[0] - 1], where_ref[spots[j]] + low // step].astype(jnp.float32)
            masked.append(pulled[:, low : low + step] * kept)
        part = sum3(nt_dot(split3(jnp.concatenate(masked, axis=1)), act))
        moved = part if moved is None else moved + part
    share = out_refs[0].shape[0]
    for i, out_ref in enumerate(out_refs):
        out_ref[...] = moved[i * share : (i + 1) * share]


def masked_step(where, spots, mask_t, column, totals, acts, scatter):
    columns, rows = sum(t.shape[0] for t in totals), totals[0].shape[1]
    outputs = 2 if scatter else 1
    shape = jax.ShapeDtypeStruct((columns // outputs, rows), jnp.float32)
    return pl.pallas_call(
        functools.partial(step_kernel, spots, len(totals)),
        out_shape=(shape,) * outputs,
        in_specs=[SMEM, SMEM, VMEM] + [VMEM] * len(totals) + [ANY] * len(acts),
        out_specs=(VMEM,) * outputs,
        scratch_shapes=[
            pltpu.VMEM((len(acts),) + acts[0].shape, acts[0].dtype),
            pltpu.SemaphoreType.DMA((len(acts),)),
        ],
        compiler_params=mib(24),
        name="masked_step",
    )(where, mask_t, column, *totals, *acts)


def finish_kernel(scale, first, spots, given, where_ref, mask_ref, initial_ref, *refs):
    sums_refs, weighted_refs, (out_ref, pieces_ref) = refs[:given], refs[given:-2], refs[-2:]
    columns = pieces_ref.shape[1]
    features = initial_ref.shape[0]
    piece = columns // len(spots)
    number = 0
    for sums_ref in sums_refs:
        for low in range(0, sums_ref.shape[0], piece):
            spot = pl.ds(pl.multiple_of(where_ref[spots[number]] * piece, piece), piece)
            value = sums_ref[low : low + piece, :]
            high = value.astype(jnp.bfloat16).astype(jnp.float32)
            rest = value - high
            middle = rest.astype(jnp.bfloat16).astype(jnp.float32)
            pieces_ref[0, spot, :] = high
            pieces_ref[1, spot, :] = middle
            pieces_ref[2, spot, :] = rest - middle
            number += 1
    pieces = pieces_ref[...].reshape(3 * columns, -1).astype(jnp.bfloat16)
    weighted = jnp.concatenate([ref[...] for ref in weighted_refs], axis=0)
    moved = sum3(nt_dot(pieces, weighted)).T * scale
    step = min(BLOCK, features)
    for low in range(0, features, step):
        for o in range(columns // BLOCK):
            kept = mask_ref[o, where_ref[first] + low // step].astype(jnp.float32)
            at = (slice(low, low + step), slice(o * BLOCK, (o + 1) * BLOCK))
            out_ref[at] = kept * (initial_ref[at] - moved[at])


def finish(where, first, spots, mask_t, initial, sums, weighted, scale):
    return pl.pallas_call(
        functools.partial(finish_kernel, scale, first, spots, len(sums)),
        out_shape=jax.ShapeDtypeStruct(initial.shape, jnp.float32),
        in_specs=[SMEM, SMEM] + [VMEM] * (1 + len(sums) + len(weighted)),
        out_specs=VMEM,
        scratch_shapes=[pltpu.VMEM((3, initial.shape[1], sums[0].shape[1]), jnp.float32)],
        compiler_params=mib(16),
        name="finish",
    )(where, mask_t, initial, *sums, *weighted)


def gram_kernel(scale, groups, panels, block, col, where_ref, *refs):
    parts = sum(len(group) for group in groups)
    weighted, acts = refs[:parts], refs[parts : parts + panels]
    out_ref, held, sems = refs[-3:]
    width = acts[0].shape[1]
    copies = []
    low = 0
    for group in groups:
        left = jnp.concatenate([weighted[i][...] for i in group], axis=0)
        height = left.shape[0]
        for j in range(panels):
            spot = 0 if panels == 1 else pl.multiple_of(jnp.bitwise_xor(where_ref[col], j) * width, width)
            held[j, low : low + height, :] = dot(left, acts[j][...]) * scale
            copy = pltpu.make_async_copy(
                held.at[j, pl.ds(low, height), :],
                out_ref.at[where_ref[block], 0, pl.ds(low, height), pl.ds(spot, width)],
                sems.at[len(copies)],
            )
            copy.start()
            copies.append(copy)
        low += height
    for copy in copies:
        copy.wait()


def gram_block(buffer, where, block, col, pieces, acts, blocks):
    rows = pieces[0].shape[1]
    features = sum(p.shape[0] for p in pieces)
    panels, width = len(acts), acts[0].shape[1]
    groups, size = [[]], 0
    for i, piece in enumerate(pieces):
        if size + piece.shape[0] > 256:
            groups.append([])
            size = 0
        groups[-1].append(i)
        size += piece.shape[0]
    operands = [where, *pieces, *acts]
    in_specs = [SMEM] + [VMEM] * (len(operands) - 1)
    aliases = {}
    if buffer is not None:
        in_specs.append(ANY)
        aliases = {len(operands): 0}
        operands.append(buffer)
    return pl.pallas_call(
        functools.partial(gram_kernel, 1.0 / rows, groups, panels, block, col),
        in_specs=in_specs,
        out_specs=ANY,
        out_shape=jax.ShapeDtypeStruct((blocks, 1, features, panels * width), jnp.float32),
        scratch_shapes=[
            pltpu.VMEM((panels, features, width), jnp.float32),
            pltpu.SemaphoreType.DMA((panels * len(groups),)),
        ],
        input_output_aliases=aliases,
        compiler_params=mib(12),
        cost_estimate=pl.CostEstimate(
            flops=2 * features * rows * panels * width,
            bytes_accessed=4 * features * panels * width,
            transcendentals=0,
        ),
    )(*operands)


def after(value, *others):
    if not others:
        return value
    return lax.optimization_barrier((value, *others))[0]


def bits(size):
    return [1 << i for i in range(size.bit_length() - 1)]


def plan(row_count, col_count, features, scatter):
    heights = [features // 2, features // 4, features // 4] if features % 64 == 0 else [features]
    half = row_count // 2
    units = []
    for step in range(1, half):
        for i in range(len(heights)):
            units.append([(i, step, 1), (i, step, -1)])
    if len(heights) == 3:
        units.append([(0, half, 1), (1, half, -1)])
        units.append([(2, half, -1)])
    else:
        units.append([(0, half, 1)])
    cols, rows = bits(col_count), bits(row_count)
    sums = [("row", bit) for bit in rows] + ([("row", 1)] if scatter else [])
    hops = [("col", bit) for bit in cols] + sums + sums
    hops += [("col", bit) for bit in reversed(cols)]
    if (row_count, col_count) == (8, 4):
        slots = SLOTS
    else:
        slots = [k * (len(hops) - 1) // len(units) for k in range(len(units))]
    return heights, units, hops, slots


def shards(activations, token_ids, initial, block_mask):
    rows, features = activations.shape
    row_count, col_count = lax.axis_size("row"), lax.axis_size("col")
    columns = initial.shape[1]
    row, col = lax.axis_index("row"), lax.axis_index("col")
    depth = row_count * col_count * features
    step_size = rows / (depth + 2.0 * math.sqrt(depth * rows) + rows)
    scatter = (columns // col_count) % 16 == 0
    heights, units, hops, slots = plan(row_count, col_count, features, scatter)
    cols = bits(col_count)
    half = row_count // 2
    mask_t = block_mask.T

    order = list(range(0, row_count, 2)) + list(range(row_count - 1, 0, -2))
    forward = [(order[i], order[(i + 1) % row_count]) for i in range(row_count)]
    backward = [(b, a) for a, b in forward]
    tail = ([("row", 1)] if scatter else []) + [("col", bit) for bit in reversed(cols)]
    table = []
    for r in range(row_count):
        for c in range(col_count):
            first_column, width = 0, columns
            for bit in cols:
                width //= 2
                first_column += (c // bit) % 2 * width
            entries = [(r * col_count + c) * features // BLOCK, c, first_column // BLOCK]
            entries += [(r * col_count + (c ^ j)) * features // BLOCK for j in range(col_count)]
            entries += [order[(order.index(r) - s) % row_count] for s in range(row_count)]
            for i in range(1 << len(tail)):
                spot = 0
                for t, (axis, bit) in enumerate(tail):
                    spot += ((r if axis == "row" else c) // bit % 2 ^ (i >> t) & 1) << t
                entries.append(spot)
            table.append(entries)
    where = jnp.array(table, jnp.int32)[row * col_count + col]
    step_spots = [3 + j for j in range(col_count)]
    source_spot = 3 + col_count
    piece_spots = [source_spot + row_count + i for i in range(1 << len(tail))]

    def mine(axis, bit):
        return jnp.bitwise_and((row if axis == "row" else col) // bit, 1).astype(jnp.int32)

    first_block = ((row * col_count + col) * features // BLOCK).astype(jnp.int32)
    keep, give, own, column, *pieces = start(
        first_block, mine("col", cols[0]), mask_t, token_ids, activations, initial, heights
    )

    arrived = {(0, i): piece for i, piece in enumerate(pieces)}

    def send_unit(k, *gate):
        for i, step, way in units[k]:
            source = arrived[((step - 1) * way % row_count, i)]
            got = lax.ppermute(after(source, *gate), "row", forward if way > 0 else backward)
            arrived[(step * way % row_count, i)] = got

    def units_at(number, *gate):
        for k, slot in enumerate(slots):
            if slot == number:
                send_unit(k, *gate)

    acts = [own]

    def gather_col(bit, *gate):
        for value in list(acts):
            acts.append(lax.ppermute(after(value, *gate), "col", [(c, c ^ bit) for c in range(col_count)]))

    def hop(number, value):
        axis, bit = hops[number]
        size = lax.axis_size(axis)
        return lax.ppermute(value, axis, [(i, i ^ bit) for i in range(size)])

    units_at(-1)
    number = 0
    for position, bit in enumerate(cols):
        gate = give
        got = hop(number, give)
        units_at(number, gate)
        if position == len(cols) - 1:
            gather_col(bit, gate)
        number += 1
        if position + 1 < len(cols) or scatter:
            keep, give = fold(keep, got, mine(*hops[number]))
        else:
            keep = keep + got
    for bit in reversed(cols[:-1]):
        gather_col(bit, keep)
    codes = [0]
    for bit in reversed(cols):
        codes += [code ^ bit for code in codes]
    acts = [acts[codes.index(j)] for j in range(col_count)]

    def row_sum(number, keep, give):
        rest = bits(row_count)
        if scatter:
            gate = give
            got = hop(number, give)
            units_at(number, gate)
            keep = keep + got
            number += 1
            rest = rest[1:]
        for _ in rest:
            gate = keep
            got = hop(number, keep)
            units_at(number, gate)
            keep = keep + got
            number += 1
        return number, keep

    number, total = row_sum(number, keep, give)
    totals = [total]
    if scatter:
        totals.append(hop(number, total))
        units_at(number, total)
        number += 1
    moved = masked_step(where, step_spots, mask_t, column, totals, acts, scatter)
    number, change = row_sum(number, moved[0], moved[-1])
    sums = [total + (total - (step_size / rows) * change)]
    for _ in tail:
        value = sums[0] if len(sums) == 1 else jnp.concatenate(sums, axis=0)
        other = hop(number, value)
        units_at(number, value)
        sums = [value, other]
        number += 1
    repaired = finish(where, 0, piece_spots, mask_t, initial, sums, pieces, step_size / rows)

    panels = acts
    if features % BLOCK:
        panels = []
        for place in range(col_count):
            chosen = acts[0]
            for j in range(1, col_count):
                chosen = jnp.where(jnp.bitwise_xor(col, j) == place, acts[j], chosen)
            panels.append(chosen)
        panels = [jnp.concatenate(panels, axis=1)]
    arrival = [0]
    for step in range(1, half + 1):
        arrival += [step] if step == half else [step, row_count - step]
    gram = None
    for slot in arrival:
        blocks = [arrived[(slot, i)] for i in range(len(heights))]
        gram = gram_block(gram, where, source_spot + slot, 1, blocks, panels, row_count)
    return gram, repaired


def solution(mesh):
    in_specs = (
        P("groups", ("row", "col")),
        P("groups"),
        P(("groups", "row", "col"), None),
        P("groups", None),
    )
    out_specs = (P("groups", "col", None, "row"), P(("groups", "row", "col"), None))
    return jax.shard_map(shards, mesh=mesh, in_specs=in_specs, out_specs=out_specs, check_vma=False)
```
